256 devices in a mesh: seqa: 4 (over x), seqb: 16 (over z, y_lo), head: 4 (over y_hi, core).
Axes of the slice: x: 4, y: 4 (y_hi: 2, y_lo: 2; y = y_hi * 2 + y_lo), z: 8, core: 2. Of those that a mesh axis runs over, the one named last changes fastest.
Arguments:
- queries: bfloat16 [32768, 4096], P(('seqa', 'seqb', 'head')), may hold values from -6 to 6
- key_vectors: bfloat16 [32768, 2048], P(('seqa', 'seqb', 'head')), may hold values from -6 to 6
- value_vectors: bfloat16 [32768, 2048], P(('seqa', 'seqb', 'head')), may hold values from -6 to 6
- output_gradient: bfloat16 [32768, 4096], P(('seqa', 'seqb', 'head')), may hold values from -6 to 6
- doc_ids: int32 [32768], replicated, may hold values from 0 to 31, as said below
Outputs:
- attn_out: bfloat16 [32768, 4096], P(('seqa', 'seqb', 'head'))
- query_grad: bfloat16 [32768, 4096], P(('seqa', 'seqb', 'head'))
- key_grad: bfloat16 [32768, 2048], P(('seqa', 'seqb', 'head'))
- value_grad: bfloat16 [32768, 2048], P(('seqa', 'seqb', 'head'))
The draws below stay inside these ranges and needn't reach their ends.
Inputs may be any that keep to these rules, and one draw needn't show every extreme that they name: `doc_ids`: ids start at 0 and never fall; every id covers whole aligned blocks of 128 tokens and the next id is one larger.
All inputs are finite; a program needn't handle non-finite values.
Results may differ from the reference program's by a relative error of at most 0.0283.
Values may be sent and summed in bfloat16 or wider, within the bound.
No kernel may reach another device: no remote copies, remote signals or barrier semaphores. Data moves between devices by JAX's collectives and lax.ppermute only.
A program may use at most 128 MiB of HBM per device.

```python
import jax
import jax.numpy as jnp
from jax import lax

HQ = 32
KEY_VALUE_HEADS = 16
HEAD_SIZE = 128
SHARD_TOKENS = 512
BLOCK = 128
QUERY_PER_KV = 2
WINDOW = 1024
DOCUMENT_TOKENS = 32768


def draw_queries(key, part):
    first_offset = jnp.clip(jax.random.normal(jax.random.fold_in(key, 1), (DOCUMENT_TOKENS, HQ * HEAD_SIZE), jnp.float32), -5.0, 5.0)
    return first_offset.astype(jnp.bfloat16)


def draw_key_vectors(key, part):
    first_offset = jnp.clip(jax.random.normal(jax.random.fold_in(key, 2), (DOCUMENT_TOKENS, KEY_VALUE_HEADS * HEAD_SIZE), jnp.float32), -5.0, 5.0)
    return first_offset.astype(jnp.bfloat16)


def draw_doc_ids(key, part):
    block_count = DOCUMENT_TOKENS // BLOCK
    doc_count = max(DOCUMENT_TOKENS // (8 * BLOCK), 1)
    order = jax.random.permutation(key, block_count - 1) + 1
    starts = jnp.zeros((block_count,), jnp.int32)
    starts = starts.at[order[:doc_count - 1]].set(1)
    starts = starts.at[0].set(1)
    doc_index = jnp.cumsum(starts) - 1
    return jnp.repeat(doc_index, BLOCK).astype(jnp.int32)


def level_of(stream_key, dims, shards, smallest, top_value):
    def one(position, shards_of):
        steps = jax.random.uniform(jax.random.fold_in(jax.random.fold_in(stream_key, 6), position), (shards_of,), jnp.float32, smallest / len(shards), top_value / len(shards))
        return jnp.repeat(jnp.exp(steps), dims[position] // shards_of).reshape((-1,) + (1,) * (len(dims) - position - 1))

    gain = one(*shards[0])
    for cut in shards[1:]:
        gain = gain * one(*cut)
    return gain


def noise(rng, extent, width, bound, shards=(), held_as=jnp.bfloat16):
    result = width * jax.random.normal(rng, extent, jnp.float32)
    if shards:
        result = result * level_of(rng, extent, shards, -0.22, 0.18)
    return jnp.clip(result, -bound, bound).astype(held_as)


def setup_inputs(seed: int = 0) -> dict:
    key_of = jax.random.split(jax.random.key(seed), 6)
    queries = draw_queries(jax.random.fold_in(key_of[5], 71), 0)
    key_vectors = draw_key_vectors(jax.random.fold_in(key_of[5], 71), 0)
    value_vectors = noise(key_of[2], (DOCUMENT_TOKENS, KEY_VALUE_HEADS * HEAD_SIZE), 1.0, 6.0, ((0, 256),))
    output_gradient = noise(key_of[3], (DOCUMENT_TOKENS, HQ * HEAD_SIZE), 1.0, 6.0, ((0, 256),))
    doc_ids = draw_doc_ids(jax.random.fold_in(key_of[5], 71), 0)
    return dict(queries=queries, key_vectors=key_vectors, value_vectors=value_vectors, output_gradient=output_gradient, doc_ids=doc_ids)


score_scale = 168.0 ** -0.5


def rounded(array):
    return lax.optimization_barrier(array.astype(jnp.bfloat16)).astype(jnp.float32)


def band_terms(block_query, block_keys, block_values, block_gradient, allowed):
    scores = score_scale * jnp.einsum("tkgd,skd->kgts", block_query, block_keys)
    masked = jnp.where(allowed, scores, -jnp.inf)
    top = jnp.max(masked, axis=-1, keepdims=True)
    total = jnp.sum(jnp.where(allowed, jnp.exp(scores - top), 0.0), axis=-1, keepdims=True)
    log_total = top + jnp.log(total)
    probs = jnp.where(allowed, jnp.exp(scores - log_total), 0.0)
    probs_low = rounded(probs)
    attended = rounded(jnp.einsum("kgts,skd->tkgd", probs_low, block_values))
    delta = jnp.einsum("tkgd,tkgd->kgt", block_gradient, attended)
    dprobs = jnp.einsum("tkgd,skd->kgts", block_gradient, block_values)
    dscores = rounded(probs * (dprobs - delta[..., None]))
    dquery = score_scale * jnp.einsum("kgts,skd->tkgd", dscores, block_keys)
    key_gradient = score_scale * jnp.einsum("kgts,tkgd->skd", dscores, block_query)
    value_gradient = jnp.einsum("kgts,tkgd->skd", probs_low, block_gradient)
    return attended, dquery, key_gradient, value_gradient


def reference(queries, key_vectors, value_vectors, output_gradient, doc_ids):
    shard_count = DOCUMENT_TOKENS // SHARD_TOKENS
    padding_rows = jnp.zeros((2 * SHARD_TOKENS, KEY_VALUE_HEADS * HEAD_SIZE), key_vectors.dtype)
    padded_keys = jnp.concatenate([padding_rows, key_vectors], axis=0)
    padded_values = jnp.concatenate([padding_rows, value_vectors], axis=0)
    pad_ids = jnp.full((2 * SHARD_TOKENS,), -1, jnp.int32)
    ids_pad = jnp.concatenate([pad_ids, doc_ids.astype(jnp.int32)])
    running_rows = DOCUMENT_TOKENS + 2 * SHARD_TOKENS

    def step(carry, shard_no):
        key_acc, value_acc = carry
        first_row = (shard_no * SHARD_TOKENS).astype(jnp.int32)
        block_query = lax.dynamic_slice_in_dim(queries, first_row, SHARD_TOKENS, 0).astype(jnp.float32).reshape(SHARD_TOKENS, KEY_VALUE_HEADS, QUERY_PER_KV, HEAD_SIZE)
        block_gradient = lax.dynamic_slice_in_dim(output_gradient, first_row, SHARD_TOKENS, 0).astype(jnp.float32).reshape(SHARD_TOKENS, KEY_VALUE_HEADS, QUERY_PER_KV, HEAD_SIZE)
        block_keys = lax.dynamic_slice_in_dim(padded_keys, first_row, 3 * SHARD_TOKENS, 0).astype(jnp.float32).reshape(3 * SHARD_TOKENS, KEY_VALUE_HEADS, HEAD_SIZE)
        block_values = lax.dynamic_slice_in_dim(padded_values, first_row, 3 * SHARD_TOKENS, 0).astype(jnp.float32).reshape(3 * SHARD_TOKENS, KEY_VALUE_HEADS, HEAD_SIZE)
        own_ids = lax.dynamic_slice_in_dim(ids_pad, first_row + 2 * SHARD_TOKENS, SHARD_TOKENS, 0)
        band_ids = lax.dynamic_slice_in_dim(ids_pad, first_row, 3 * SHARD_TOKENS, 0)
        own_pos = first_row + jnp.arange(SHARD_TOKENS, dtype=jnp.int32)
        band_pos = first_row - 2 * SHARD_TOKENS + jnp.arange(3 * SHARD_TOKENS, dtype=jnp.int32)
        offset = own_pos[:, None] - band_pos[None, :]
        allowed = (offset >= 0) & (offset < WINDOW) & (own_ids[:, None] == band_ids[None, :])
        attended, dquery, key_gradient, value_gradient = band_terms(block_query, block_keys, block_values, block_gradient, allowed)
        key_gradient = key_gradient.reshape(3 * SHARD_TOKENS, KEY_VALUE_HEADS * HEAD_SIZE)
        value_gradient = value_gradient.reshape(3 * SHARD_TOKENS, KEY_VALUE_HEADS * HEAD_SIZE)
        key_add = jnp.concatenate([rounded(key_gradient[:2 * SHARD_TOKENS]), key_gradient[2 * SHARD_TOKENS:]], axis=0)
        value_add = jnp.concatenate([rounded(value_gradient[:2 * SHARD_TOKENS]), value_gradient[2 * SHARD_TOKENS:]], axis=0)
        key_acc = lax.dynamic_update_slice_in_dim(key_acc, lax.dynamic_slice_in_dim(key_acc, first_row, 3 * SHARD_TOKENS, 0) + key_add, first_row, 0)
        value_acc = lax.dynamic_update_slice_in_dim(value_acc, lax.dynamic_slice_in_dim(value_acc, first_row, 3 * SHARD_TOKENS, 0) + value_add, first_row, 0)
        return (key_acc, value_acc), (attended.reshape(SHARD_TOKENS, HQ * HEAD_SIZE), dquery.reshape(SHARD_TOKENS, HQ * HEAD_SIZE))

    initial_running = (jnp.zeros((running_rows, KEY_VALUE_HEADS * HEAD_SIZE), jnp.float32), jnp.zeros((running_rows, KEY_VALUE_HEADS * HEAD_SIZE), jnp.float32))
    (key_acc, value_acc), (attended, dquery) = lax.scan(step, initial_running, jnp.arange(shard_count, dtype=jnp.int32))
    attn_out = attended.reshape(DOCUMENT_TOKENS, HQ * HEAD_SIZE).astype(jnp.bfloat16)
    query_grad = dquery.reshape(DOCUMENT_TOKENS, HQ * HEAD_SIZE).astype(jnp.bfloat16)
    key_grad = key_acc[2 * SHARD_TOKENS:].astype(jnp.bfloat16)
    value_grad = value_acc[2 * SHARD_TOKENS:].astype(jnp.bfloat16)
    return (attn_out, query_grad, key_grad, value_grad)
```

```python
import jax
import jax.numpy as jnp
import numpy as np
from jax import lax
from jax.experimental import pallas as pl
from jax.experimental.pallas import tpu as pltpu
from jax.sharding import Mesh, PartitionSpec as P

HEAD_SIZE = 128
BLOCK = 128
TILE = 256
SLAB = 1024
NEG = -1e30

score_scale = 168.0 ** (-0.5)
exp2_scale = score_scale * 1.4426950408889634

NT = (((1,), (1,)), ((), ()))
NN = (((1,), (0,)), ((), ()))


def dot(a, b, dims=NN):
    return lax.dot_general(a, b, dims, preferred_element_type=jnp.float32)


def run_copies(copies):
    for copy in copies:
        copy.start()
    for copy in copies:
        copy.wait()


def pack_kv_kernel(k_ref, v_ref, out_ref, sem):
    run_copies([
        pltpu.make_async_copy(
            src.at[:, pl.ds(256 * g, 256)], out_ref.at[g, :, pl.ds(256 * n, 256)], sem.at[2 * g + n]
        )
        for g in range(8)
        for n, src in enumerate((k_ref, v_ref))
    ])


def pack_qd_kernel(q_ref, d_ref, out0_ref, out1_ref, sem):
    run_copies([
        pltpu.make_async_copy(
            src.at[:, pl.ds(512 * g + 256 * c, 256)],
            out.at[g, :, pl.ds(256 * n, 256)],
            sem.at[4 * g + 2 * c + n],
        )
        for c, out in enumerate((out0_ref, out1_ref))
        for g in range(8)
        for n, src in enumerate((q_ref, d_ref))
    ])


ANY = pl.BlockSpec(memory_space=pl.ANY)


def pack_kv(k, v):
    rows = k.shape[0]
    return pl.pallas_call(
        pack_kv_kernel,
        out_shape=jax.ShapeDtypeStruct((8, rows, 512), k.dtype),
        in_specs=[ANY, ANY],
        out_specs=ANY,
        scratch_shapes=[pltpu.SemaphoreType.DMA((16,))],
        cost_estimate=pl.CostEstimate(flops=0, transcendentals=0, bytes_accessed=2 << 20),
        name="pack_kv",
    )(k, v)


def pack_qd(q, d):
    rows = q.shape[0]
    shape = jax.ShapeDtypeStruct((8, rows, 512), q.dtype)
    return pl.pallas_call(
        pack_qd_kernel,
        out_shape=(shape, shape),
        in_specs=[ANY, ANY],
        out_specs=(ANY, ANY),
        scratch_shapes=[pltpu.SemaphoreType.DMA((32,))],
        cost_estimate=pl.CostEstimate(flops=0, transcendentals=0, bytes_accessed=4 << 20),
        name="pack_qd",
    )(q, d)


def unpack_kernel(a0_ref, a1_ref, kv_ref, o_ref, dq_ref, dk_ref, dv_ref, sem):
    copies = []
    for g in range(8):
        for c, src in enumerate((a0_ref, a1_ref)):
            for n, out in enumerate((o_ref, dq_ref)):
                copies.append((
                    src.at[g, :, pl.ds(256 * n, 256)],
                    out.at[:, pl.ds(512 * g + 256 * c, 256)],
                ))
        for n, out in enumerate((dk_ref, dv_ref)):
            copies.append((kv_ref.at[g, :, pl.ds(256 * n, 256)], out.at[:, pl.ds(256 * g, 256)]))
    run_copies([
        pltpu.make_async_copy(src, dst, sem.at[n]) for n, (src, dst) in enumerate(copies)
    ])


def unpack(a0, a1, kv):
    rows = a0.shape[1]
    wide = jax.ShapeDtypeStruct((rows, 4096), a0.dtype)
    narrow = jax.ShapeDtypeStruct((rows, 2048), a0.dtype)
    return pl.pallas_call(
        unpack_kernel,
        out_shape=(wide, wide, narrow, narrow),
        in_specs=[ANY] * 3,
        out_specs=(ANY,) * 4,
        scratch_shapes=[pltpu.SemaphoreType.DMA((48,))],
        cost_estimate=pl.CostEstimate(flops=0, transcendentals=0, bytes_accessed=6 << 20),
        name="unpack",
    )(a0, a1, kv)


def attn_kernel(
    bias_ref, qd_ref, kh_ref, vh_ref, ko_ref, vo_ref,
    out_ref, ghalo_ref, gown_ref,
    kaug, vaug, kt, v1t, qaug, doaug, s_ref, e_ref, d_ref, dk_acc, dv_acc,
):
    i = pl.program_id(0)
    f32, bf16 = jnp.float32, jnp.bfloat16

    @pl.when(i == 0)
    def _():
        lane = lax.broadcasted_iota(jnp.int32, (TILE, 128), 1)
        row = lax.broadcasted_iota(jnp.int32, (TILE, 128), 0)
        three = jnp.where(lane < 3, 1.0, 0.0).astype(bf16)
        for half, (k_ref, v_ref) in enumerate(((kh_ref, vh_ref), (ko_ref, vo_ref))):
            for n in range(SLAB // TILE):
                src = slice(TILE * n, TILE * (n + 1))
                at = SLAB * half + TILE * n
                dst = slice(at, at + TILE)
                k = k_ref[src, :]
                v = v_ref[src, :]
                kaug[dst, 0:128] = k
                kaug[dst, 128:256] = jnp.where(lane == (row + at) // BLOCK, 1.0, 0.0).astype(bf16)
                vaug[dst, 0:128] = v
                vaug[dst, 128:256] = three
                kt[:, dst] = k.T
                v1t[0:128, dst] = v.T
                v1t[128:144, dst] = jnp.ones((16, TILE), bf16)

    base = pl.multiple_of(i * TILE, TILE)
    window = pl.ds(base, 5 * TILE)

    for b in range(2):
        row_bias = bias_ref[pl.ds(2 * i + b, 1), :]
        rows_bias = jnp.broadcast_to(row_bias, (BLOCK, 128)).astype(bf16)
        for h in range(2):
            qaug[TILE * h + BLOCK * b : TILE * h + BLOCK * (b + 1), 128:256] = rows_bias
    for h in range(2):
        qaug[TILE * h : TILE * (h + 1), 0:128] = qd_ref[:, 128 * h : 128 * (h + 1)]

    s_pos = lax.broadcasted_iota(jnp.int32, (TILE, TILE), 0)
    t_pos = lax.broadcasted_iota(jnp.int32, (TILE, TILE), 1)
    far = s_pos > t_pos
    top8 = jnp.full((8, 2 * TILE), NEG, f32)
    for j in range(5):
        s = dot(kaug[pl.ds(base + TILE * j, TILE), :], qaug[...], NT)
        if j in (0, 4):
            keep = far if j == 0 else jnp.logical_not(far)
            s = jnp.concatenate(
                [jnp.where(keep, s[:, :TILE], NEG), jnp.where(keep, s[:, TILE:], NEG)], axis=1
            )
        s_ref[TILE * j : TILE * (j + 1), :] = s
        top8 = jnp.maximum(top8, jnp.max(s.reshape(TILE // 8, 8, 2 * TILE), axis=0))
    top = jnp.max(top8, axis=0, keepdims=True)
    for j in range(5):
        rows = slice(TILE * j, TILE * (j + 1))
        e_ref[rows, :] = jnp.exp2((s_ref[rows, :] - top) * exp2_scale).astype(bf16)

    ot = dot(v1t[:, window], e_ref[...])
    r = 1.0 / ot[128:129, :]
    attended = (ot[0:128, :] * r).T.astype(bf16)
    r_rows = jnp.broadcast_to(r, (128, 2 * TILE)).T
    grad = jnp.concatenate([qd_ref[:, 256:384], qd_ref[:, 384:512]], axis=0)
    grad_n = (grad.astype(f32) * r_rows).astype(bf16)
    delta = jnp.sum(grad_n.astype(f32) * attended.astype(f32), axis=1, keepdims=True)
    minus = jnp.broadcast_to(-delta, (2 * TILE, 128))
    part0 = minus.astype(bf16).astype(f32)
    part1 = (minus - part0).astype(bf16).astype(f32)
    part2 = minus - part0 - part1
    lane = lax.broadcasted_iota(jnp.int32, (2 * TILE, 128), 1)
    parts = jnp.where(
        lane == 0, part0, jnp.where(lane == 1, part1, jnp.where(lane == 2, part2, 0.0))
    )
    doaug[:, 0:128] = grad_n
    doaug[:, 128:256] = parts.astype(bf16)
    for h in range(2):
        out_ref[:, 128 * h : 128 * (h + 1)] = attended[TILE * h : TILE * (h + 1), :]

    for j in range(5):
        rows = slice(TILE * j, TILE * (j + 1))
        dp = dot(vaug[pl.ds(base + TILE * j, TILE), :], doaug[...], NT)
        d_ref[rows, :] = (e_ref[rows, :].astype(f32) * dp).astype(bf16)

    dq = (dot(kt[:, window], d_ref[...]) * score_scale).T.astype(bf16)
    for h in range(2):
        out_ref[:, 256 + 128 * h : 384 + 128 * h] = dq[TILE * h : TILE * (h + 1), :]
    dv = dot(e_ref[...], doaug[:, 0:128])
    dk = dot(d_ref[...], qaug[:, 0:128])

    @pl.when(i == 0)
    def _():
        dk_acc[0 : 5 * TILE, :] = dk
        dv_acc[0 : 5 * TILE, :] = dv

    @pl.when(i > 0)
    def _():
        old = pl.ds(base, 4 * TILE)
        new = pl.ds(base + 4 * TILE, TILE)
        dk_acc[old, :] = dk_acc[old, :] + dk[0 : 4 * TILE, :]
        dv_acc[old, :] = dv_acc[old, :] + dv[0 : 4 * TILE, :]
        dk_acc[new, :] = dk[4 * TILE :, :]
        dv_acc[new, :] = dv[4 * TILE :, :]

    ghalo_ref[:, 0:128] = (dk_acc[pl.ds(base, TILE), :] * score_scale).astype(bf16)
    ghalo_ref[:, 128:256] = dv_acc[pl.ds(base, TILE), :].astype(bf16)

    @pl.when(i == SLAB // TILE - 1)
    def _():
        gown_ref[:, 0:128] = dk_acc[SLAB : 2 * SLAB, :] * score_scale
        gown_ref[:, 128:256] = dv_acc[SLAB : 2 * SLAB, :]


def attend(bias, qd, kv_halo, kv_own, chunk):
    f32, bf16 = jnp.float32, jnp.bfloat16
    steps = SLAB // TILE

    def whole(cols, at):
        return pl.BlockSpec((SLAB, cols), lambda i: (0, at), pipeline_mode=pl.Buffered(1))

    return pl.pallas_call(
        attn_kernel,
        grid=(steps,),
        out_shape=(
            jax.ShapeDtypeStruct((SLAB, 512), bf16),
            jax.ShapeDtypeStruct((SLAB, 256), bf16),
            jax.ShapeDtypeStruct((SLAB, 256), f32),
        ),
        in_specs=[
            pl.BlockSpec((8, 128), lambda i: (0, 0)),
            pl.BlockSpec((TILE, 512), lambda i: (i, 0)),
            whole(128, chunk),
            whole(128, 2 + chunk),
            whole(128, chunk),
            whole(128, 2 + chunk),
        ],
        out_specs=(
            pl.BlockSpec((TILE, 512), lambda i: (i, 0)),
            pl.BlockSpec((TILE, 256), lambda i: (i, 0)),
            pl.BlockSpec((SLAB, 256), lambda i: (0, 0), pipeline_mode=pl.Buffered(1)),
        ),
        scratch_shapes=[
            pltpu.VMEM((2 * SLAB, 256), bf16),
            pltpu.VMEM((2 * SLAB, 256), bf16),
            pltpu.VMEM((128, 2 * SLAB), bf16),
            pltpu.VMEM((144, 2 * SLAB), bf16),
            pltpu.VMEM((2 * TILE, 256), bf16),
            pltpu.VMEM((2 * TILE, 256), bf16),
            pltpu.VMEM((5 * TILE, 2 * TILE), f32),
            pltpu.VMEM((5 * TILE, 2 * TILE), bf16),
            pltpu.VMEM((5 * TILE, 2 * TILE), bf16),
            pltpu.VMEM((2 * SLAB, 128), f32),
            pltpu.VMEM((2 * SLAB, 128), f32),
        ],
        compiler_params=pltpu.CompilerParams(
            dimension_semantics=("arbitrary",), vmem_limit_bytes=40 << 20
        ),
        cost_estimate=pl.CostEstimate(
            flops=14 * 10**9, transcendentals=3 * 10**6, bytes_accessed=6 << 20
        ),
        name=f"attend_{chunk}",
    )(bias, qd, kv_halo, kv_halo, kv_own, kv_own)


def block_bias(doc_ids, slab):
    blocks = SLAB // BLOCK
    padded = jnp.concatenate([jnp.full((SLAB,), -1, jnp.int32), doc_ids])
    ids = lax.dynamic_slice_in_dim(padded, slab * SLAB, 2 * SLAB, 0).reshape(2 * blocks, BLOCK)[:, 0]
    own = ids[blocks:]
    query = jnp.arange(blocks)[:, None]
    key = jnp.arange(2 * blocks)[None, :]
    ok = (own[:, None] == ids[None, :]) & (key >= query) & (key <= query + blocks)
    return jnp.pad(jnp.where(ok, 0.0, NEG).astype(jnp.float32), ((0, 0), (0, 128 - 2 * blocks)))


GROUP = ("y_lo", "head")
LINE = ("x", "z")


def exchange(x):
    return lax.all_to_all(x, GROUP, split_axis=0, concat_axis=0, tiled=False)


def shifted(x, by):
    count = lax.axis_size(LINE)
    pairs = [(i, i + by) for i in range(count) if 0 <= i + by < count]
    return lax.ppermute(x, LINE, pairs)


def body(queries, key_vectors, value_vectors, output_gradient, doc_ids):
    kv_send = pack_kv(key_vectors, value_vectors)
    kv_own = exchange(kv_send).reshape(SLAB, 512)
    qd_send = pack_qd(queries, output_gradient)
    bias = block_bias(doc_ids, lax.axis_index(LINE))
    kv_halo = shifted(kv_own, 1)
    out_send = []
    grads = []
    for chunk in range(2):
        qd = exchange(qd_send[chunk]).reshape(SLAB, 512)
        out, g_halo, g_own = attend(bias, qd, kv_halo, kv_own, chunk)
        out_send.append(out.reshape(8, 128, 512))
        grads.append(g_own + shifted(g_halo, -1).astype(jnp.float32))
    total = jnp.concatenate(
        [grads[0][:, :128], grads[1][:, :128], grads[0][:, 128:], grads[1][:, 128:]], axis=1
    ).astype(jnp.bfloat16).reshape(8, 128, 512)
    received = [exchange(x) for x in out_send]
    return unpack(received[0], received[1], exchange(total))


def solution(mesh):
    seqa, seqb, head = (mesh.shape[a] for a in ("seqa", "seqb", "head"))
    fine = Mesh(mesh.devices.reshape(seqa, seqb // 2, 2, head), ("x", "z", "y_lo", "head"))
    tokens = P(("x", "z", "y_lo", "head"), None)
    return jax.shard_map(
        body, mesh=fine, in_specs=(tokens,) * 4 + (P(),), out_specs=(tokens,) * 4, check_vma=False
    )
```

```python
import functools

import jax
import jax.numpy as jnp
from jax import lax
from jax.experimental import pallas as pl
from jax.experimental.pallas import tpu as pltpu
from jax.sharding import Mesh, PartitionSpec as P

HEAD_SIZE = 128
BLOCK = 128
TILE = 256
SLAB = 1024
NEG = -1e30
GRANT = 12
GRANT_ATTEND = 28

score_scale = 168.0 ** (-0.5)
exp2_scale = score_scale * 1.4426950408889634

NT = (((1,), (1,)), ((), ()))
NN = (((1,), (0,)), ((), ()))


def dot(a, b, dims=NN):
    return lax.dot_general(a, b, dims, preferred_element_type=jnp.float32)


SRC, DST, CORE = 0, 4, 8


def scalars():
    y = lax.axis_index("y_hi") * 2 + lax.axis_index("y_lo")
    tiles = []
    for by in (0, -1, -2, -3, 0, 1, 2, 3):
        chip = (y + by) % 4
        tiles.append((chip % 2) * 2 + chip // 2)
    return jnp.stack(tiles + [lax.axis_index("core")]).astype(jnp.int32)


def aligned(start, size):
    return pl.ds(pl.multiple_of(start, 128), size)


def local_call(kernel, out_shape, name, grant, cost, scratch=()):
    def call(tab, *args):
        return pl.pallas_call(
            kernel,
            out_shape=out_shape,
            in_specs=[pl.BlockSpec(memory_space=pltpu.SMEM)]
            + [pl.BlockSpec(memory_space=pltpu.VMEM)] * len(args),
            out_specs=jax.tree.map(lambda _: pl.BlockSpec(memory_space=pltpu.VMEM), out_shape),
            scratch_shapes=list(scratch),
            compiler_params=pltpu.CompilerParams(vmem_limit_bytes=grant << 20),
            cost_estimate=cost,
            name=name,
        )(tab, *args)

    return call


def moves(megabytes):
    return pl.CostEstimate(flops=0, transcendentals=0, bytes_accessed=int(megabytes * 2**20))


def array(*shape, dtype=jnp.bfloat16):
    return jax.ShapeDtypeStruct(shape, dtype)


def pack_kv_kernel(tab, k_ref, v_ref, *out):
    for i in range(4):
        at = tab[DST + i] * 512
        for n, src in enumerate((k_ref, v_ref)):
            for head in range(4):
                col = 256 * head + 128 * n
                out[i][:, col : col + 128] = src[:, aligned(at + 128 * head, 128)]


def pack_qd_kernel(tab, q_ref, d_ref, *out):
    for i in range(4):
        at = tab[DST + i] * 1024
        for n, src in enumerate((q_ref, d_ref)):
            for core in range(2):
                for chunk in range(2):
                    col = 512 * core + 256 * n
                    out[4 * chunk + i][:, col : col + 256] = src[
                        :, aligned(at + 512 * core + 256 * chunk, 256)
                    ]


def to_sibling_in_kernel(tab, p0, p1, p2, p3, out):
    at = (1 - tab[CORE]) * 512
    for i, p in enumerate((p0, p1, p2, p3)):
        out[i] = p[:, aligned(at, 512)]


def to_sibling_out_kernel(tab, p0, p1, p2, p3, out):
    at = (1 - tab[CORE]) * 128
    for i, p in enumerate((p0, p1, p2, p3)):
        out[i] = p[aligned(at, 128), :]


def halo_kernel(tab, p0, p1, p2, p3, sib, out0, out1):
    at = tab[CORE] * 512
    for chunk, out in enumerate((out0, out1)):
        for i, p in enumerate((p0, p1, p2, p3)):
            out[2 * i] = p[:, aligned(at + 256 * chunk, 256)]
            out[2 * i + 1] = sib[i, :, 256 * chunk : 256 * (chunk + 1)]


def merge_kernel(tab, own0, own1, from0, from1, *out):
    for i in range(4):
        rows = aligned(tab[DST + i] * TILE, TILE)
        for chunk, (own, other) in enumerate(((own0, from0), (own1, from1))):
            out[i][:, 256 * chunk : 256 * (chunk + 1)] = (
                own[rows, :] + other[rows, :].astype(jnp.float32)
            ).astype(jnp.bfloat16)


def arrived(tab, direct, sib):
    core = tab[CORE]
    for i in range(4):
        yield 2 * tab[SRC + i] + core, direct[i].at[aligned(core * 128, 128), :]
        yield 2 * tab[SRC + i] + 1 - core, sib.at[i]


def unpack_out_kernel(tab, *refs):
    o_ref, dq_ref = refs[10:]
    for chunk in range(2):
        parts = refs[5 * chunk : 5 * chunk + 5]
        for group, piece in arrived(tab, parts[:4], parts[4]):
            for n, out in enumerate((o_ref, dq_ref)):
                out[:, aligned(group * 512 + 256 * chunk, 256)] = piece[:, 256 * n : 256 * (n + 1)]


def unpack_kv_kernel(tab, p0, p1, p2, p3, sib, dk_ref, dv_ref):
    for group, piece in arrived(tab, (p0, p1, p2, p3), sib):
        for chunk in range(2):
            for n, out in enumerate((dk_ref, dv_ref)):
                at = 256 * chunk + 128 * n
                out[:, aligned(group * 256 + 128 * chunk, 128)] = piece[:, at : at + 128]


def attn_kernel(chunk, tab, bias_ref, *refs):
    q_parts, q_sib, kv_parts, kv_sib, halo = refs[0:4], refs[4], refs[5:9], refs[9], refs[10]
    outs, ghalo_ref, gown_ref = refs[11:15], refs[15], refs[16]
    (
        kaug, vaug, kt, v1t, qd_ref, out_ref, qaug, doaug, s_ref, e_ref, d_ref, dk_acc, dv_acc,
    ) = refs[17:]
    f32, bf16 = jnp.float32, jnp.bfloat16
    core = tab[CORE]

    lane = lax.broadcasted_iota(jnp.int32, (BLOCK, 128), 1)
    three = jnp.where(lane < 3, 1.0, 0.0).astype(bf16)

    def place_kv(at, k, v):
        rows = aligned(at, BLOCK)
        kaug[rows, 0:128] = k
        kaug[rows, 128:256] = jnp.where(lane == at // BLOCK, 1.0, 0.0).astype(bf16)
        vaug[rows, 0:128] = v
        vaug[rows, 128:256] = three
        kt[:, rows] = k.T
        v1t[0:128, rows] = v.T
        v1t[128:144, rows] = jnp.ones((16, BLOCK), bf16)

    for i in range(4):
        for n in range(2):
            at = tab[SRC + i] * TILE + (core if n == 0 else 1 - core) * BLOCK
            place_kv(at, halo[2 * i + n, :, 0:128], halo[2 * i + n, :, 128:256])
            if n == 0:
                col = core * 512 + 256 * chunk
                k = kv_parts[i][:, aligned(col, 128)]
                v = kv_parts[i][:, aligned(col + 128, 128)]
                qd = q_parts[i][:, aligned(core * 512, 512)]
            else:
                k = kv_sib[i, :, 256 * chunk : 256 * chunk + 128]
                v = kv_sib[i, :, 256 * chunk + 128 : 256 * chunk + 256]
                qd = q_sib[i]
            place_kv(SLAB + at, k, v)
            qd_ref[aligned(at, BLOCK), :] = qd
    dk_acc[...] = jnp.zeros_like(dk_acc)
    dv_acc[...] = jnp.zeros_like(dv_acc)

    @pl.loop(0, SLAB // TILE)
    def _(i):
        tile = pl.ds(pl.multiple_of(i * TILE, TILE), TILE)
        attn_tile(
            i, bias_ref, qd_ref.at[tile, :], out_ref.at[tile, :],
            kaug, vaug, kt, v1t, qaug, doaug, s_ref, e_ref, d_ref, dk_acc, dv_acc,
        )

    for i in range(4):
        outs[i][...] = out_ref[aligned(tab[DST + i] * TILE, TILE), :]
    ghalo_ref[:, 0:128] = (dk_acc[0:SLAB, :] * score_scale).astype(bf16)
    ghalo_ref[:, 128:256] = dv_acc[0:SLAB, :].astype(bf16)
    gown_ref[:, 0:128] = dk_acc[SLAB : 2 * SLAB, :] * score_scale
    gown_ref[:, 128:256] = dv_acc[SLAB : 2 * SLAB, :]


def attn_tile(
    i, bias_ref, qd_ref, out_ref,
    kaug, vaug, kt, v1t, qaug, doaug, s_ref, e_ref, d_ref, dk_acc, dv_acc,
):
    f32, bf16 = jnp.float32, jnp.bfloat16
    base = pl.multiple_of(i * TILE, TILE)
    window = pl.ds(base, 5 * TILE)

    for b in range(2):
        row_bias = bias_ref[pl.ds(2 * i + b, 1), :]
        rows_bias = jnp.broadcast_to(row_bias, (BLOCK, 128)).astype(bf16)
        for h in range(2):
            qaug[TILE * h + BLOCK * b : TILE * h + BLOCK * (b + 1), 128:256] = rows_bias
    for h in range(2):
        qaug[TILE * h : TILE * (h + 1), 0:128] = qd_ref[:, 128 * h : 128 * (h + 1)]

    s_pos = lax.broadcasted_iota(jnp.int32, (TILE, TILE), 0)
    t_pos = lax.broadcasted_iota(jnp.int32, (TILE, TILE), 1)
    far = s_pos > t_pos
    top8 = jnp.full((8, 2 * TILE), NEG, f32)
    for j in range(5):
        s = dot(kaug[pl.ds(base + TILE * j, TILE), :], qaug[...], NT)
        if j in (0, 4):
            keep = far if j == 0 else jnp.logical_not(far)
            s = jnp.concatenate(
                [jnp.where(keep, s[:, :TILE], NEG), jnp.where(keep, s[:, TILE:], NEG)], axis=1
            )
        s_ref[TILE * j : TILE * (j + 1), :] = s
        top8 = jnp.maximum(top8, jnp.max(s.reshape(TILE // 8, 8, 2 * TILE), axis=0))
    top = jnp.max(top8, axis=0, keepdims=True)
    for j in range(5):
        rows = slice(TILE * j, TILE * (j + 1))
        e_ref[rows, :] = jnp.exp2((s_ref[rows, :] - top) * exp2_scale).astype(bf16)

    ot = dot(v1t[:, window], e_ref[...])
    r = 1.0 / ot[128:129, :]
    attended = (ot[0:128, :] * r).T.astype(bf16)
    r_rows = jnp.broadcast_to(r, (128, 2 * TILE)).T
    grad = jnp.concatenate([qd_ref[:, 256:384], qd_ref[:, 384:512]], axis=0)
    grad_n = (grad.astype(f32) * r_rows).astype(bf16)
    delta = jnp.sum(grad_n.astype(f32) * attended.astype(f32), axis=1, keepdims=True)
    minus = jnp.broadcast_to(-delta, (2 * TILE, 128))
    part0 = minus.astype(bf16).astype(f32)
    part1 = (minus - part0).astype(bf16).astype(f32)
    part2 = minus - part0 - part1
    lane = lax.broadcasted_iota(jnp.int32, (2 * TILE, 128), 1)
    parts = jnp.where(
        lane == 0, part0, jnp.where(lane == 1, part1, jnp.where(lane == 2, part2, 0.0))
    )
    doaug[:, 0:128] = grad_n
    doaug[:, 128:256] = parts.astype(bf16)
    for h in range(2):
        out_ref[:, 128 * h : 128 * (h + 1)] = attended[TILE * h : TILE * (h + 1), :]

    for j in range(5):
        rows = slice(TILE * j, TILE * (j + 1))
        dp = dot(vaug[pl.ds(base + TILE * j, TILE), :], doaug[...], NT)
        d_ref[rows, :] = (e_ref[rows, :].astype(f32) * dp).astype(bf16)

    dq = (dot(kt[:, window], d_ref[...]) * score_scale).T.astype(bf16)
    for h in range(2):
        out_ref[:, 256 + 128 * h : 384 + 128 * h] = dq[TILE * h : TILE * (h + 1), :]
    dv = dot(e_ref[...], doaug[:, 0:128])
    dk = dot(d_ref[...], qaug[:, 0:128])

    dk_acc[window, :] = dk_acc[window, :] + dk
    dv_acc[window, :] = dv_acc[window, :] + dv


def attend(chunk, tab, bias, q_parts, q_sib, kv_parts, kv_sib, halo):
    f32, bf16 = jnp.float32, jnp.bfloat16
    call = local_call(
        functools.partial(attn_kernel, chunk),
        [array(TILE, 512)] * 4 + [array(SLAB, 256), array(SLAB, 256, dtype=f32)],
        f"attend_{chunk}",
        GRANT_ATTEND,
        pl.CostEstimate(flops=14 * 10**9, transcendentals=0, bytes_accessed=4 << 20),
        scratch=[
            pltpu.VMEM((2 * SLAB, 256), bf16),
            pltpu.VMEM((2 * SLAB, 256), bf16),
            pltpu.VMEM((128, 2 * SLAB), bf16),
            pltpu.VMEM((144, 2 * SLAB), bf16),
            pltpu.VMEM((SLAB, 512), bf16),
            pltpu.VMEM((SLAB, 512), bf16),
            pltpu.VMEM((2 * TILE, 256), bf16),
            pltpu.VMEM((2 * TILE, 256), bf16),
            pltpu.VMEM((5 * TILE, 2 * TILE), f32),
            pltpu.VMEM((5 * TILE, 2 * TILE), bf16),
            pltpu.VMEM((5 * TILE, 2 * TILE), bf16),
            pltpu.VMEM((2 * SLAB, 128), f32),
            pltpu.VMEM((2 * SLAB, 128), f32),
        ],
    )
    out = call(tab, bias, *q_parts, q_sib, *kv_parts, kv_sib, halo)
    return out[:4], out[4], out[5]


def block_bias(doc_ids, slab):
    blocks = SLAB // BLOCK
    padded = jnp.concatenate([jnp.full((SLAB,), -1, jnp.int32), doc_ids])
    ids = lax.dynamic_slice_in_dim(padded, slab * SLAB, 2 * SLAB, 0).reshape(2 * blocks, BLOCK)[:, 0]
    own = ids[blocks:]
    query = jnp.arange(blocks)[:, None]
    key = jnp.arange(2 * blocks)[None, :]
    ok = (own[:, None] == ids[None, :]) & (key >= query) & (key <= query + blocks)
    return jnp.pad(jnp.where(ok, 0.0, NEG).astype(jnp.float32), ((0, 0), (0, 128 - 2 * blocks)))


RING = ("y_lo", "y_hi", "core")
LINE = ("x", "z")


def ring_shift(x, by):
    pairs = []
    for device in range(8):
        y_lo, y_hi, core = device // 4, device // 2 % 2, device % 2
        chip = (2 * y_hi + y_lo + by) % 4
        pairs.append((device, (chip % 2) * 4 + (chip // 2) * 2 + core))
    return lax.ppermute(x, RING, pairs)


def spread(pieces):
    return [pieces[0]] + [ring_shift(pieces[i], i) for i in (1, 3, 2)]


def in_order(received):
    return [received[0], received[1], received[3], received[2]]


def exchange(pieces):
    return in_order(spread(pieces))


def swap_cores(x):
    return lax.ppermute(x, "core", [(0, 1), (1, 0)])


def shifted(x, by):
    count = lax.axis_size(LINE)
    pairs = [(i, i + by) for i in range(count) if 0 <= i + by < count]
    return lax.ppermute(x, LINE, pairs)


def body(queries, key_vectors, value_vectors, output_gradient, doc_ids):
    tab = scalars()
    rows = queries.shape[0]
    sibling_in = local_call(
        to_sibling_in_kernel, array(4, rows, 512), "to_sibling_in", GRANT, moves(1)
    )
    sibling_out = local_call(
        to_sibling_out_kernel, array(4, rows, 512), "to_sibling_out", GRANT, moves(1)
    )
    kv_send = local_call(
        pack_kv_kernel, [array(rows, 1024)] * 4, "pack_kv", GRANT, moves(2)
    )(tab, key_vectors, value_vectors)
    qd_send = local_call(
        pack_qd_kernel, [array(rows, 1024)] * 8, "pack_qd", GRANT, moves(4)
    )(tab, queries, output_gradient)
    bias = block_bias(doc_ids, lax.axis_index(LINE))

    kv = exchange(kv_send)
    kv_sib = swap_cores(sibling_in(tab, *kv))
    halo_send = local_call(
        halo_kernel, [array(8, rows, 256)] * 2, "halo", GRANT, moves(2)
    )(tab, *kv, kv_sib)
    halo = [shifted(x, 1) for x in halo_send]
    out, own, other = [], [], []
    for chunk in range(2):
        qd = exchange(qd_send[4 * chunk : 4 * chunk + 4])
        qd_sib = swap_cores(sibling_in(tab, *qd))
        pieces, g_halo, g_own = attend(chunk, tab, bias, qd, qd_sib, kv, kv_sib, halo[chunk])
        received = exchange(pieces)
        out += [*received, swap_cores(sibling_out(tab, *received))]
        own.append(g_own)
        other.append(shifted(g_halo, -1))
    attn_out, query_grad = local_call(
        unpack_out_kernel, [array(rows, 4096)] * 2, "unpack_out", GRANT, moves(4)
    )(tab, *out)
    pieces = local_call(merge_kernel, [array(TILE, 512)] * 4, "merge", GRANT, moves(4))(
        tab, *own, *other
    )
    received = exchange(pieces)
    key_grad, value_grad = local_call(
        unpack_kv_kernel, [array(rows, 2048)] * 2, "unpack_kv", GRANT, moves(2)
    )(tab, *received, swap_cores(sibling_out(tab, *received)))
    return attn_out, query_grad, key_grad, value_grad


def solution(mesh):
    seqa, seqb, head = (mesh.shape[a] for a in ("seqa", "seqb", "head"))
    axes = ("x", "z", "y_lo", "y_hi", "core")
    fine = Mesh(mesh.devices.reshape(seqa, seqb // 2, 2, head // 2, 2), axes)
    tokens = P(axes, None)
    return jax.shard_map(
        body, mesh=fine, in_specs=(tokens,) * 4 + (P(),), out_specs=(tokens,) * 4, check_vma=False
    )
```

```python
import functools

import jax
import jax.numpy as jnp
from jax import lax
from jax.experimental import pallas as pl
from jax.experimental.pallas import tpu as pltpu
from jax.sharding import Mesh, PartitionSpec as P

HEAD_SIZE = 128
BLOCK = 128
TILE = 256
SLAB = 1024
NEG = -1e30
GRANT = 12
GRANT_ATTEND = 28

score_scale = 168.0 ** (-0.5)
exp2_scale = score_scale * 1.4426950408889634

NT = (((1,), (1,)), ((), ()))
NN = (((1,), (0,)), ((), ()))


def dot(a, b, dims=NN):
    return lax.dot_general(a, b, dims, preferred_element_type=jnp.float32)


SRC, DST, CORE = 0, 4, 8


def scalars():
    y = lax.axis_index("y_hi") * 2 + lax.axis_index("y_lo")
    tiles = []
    for by in (0, -1, -2, -3, 0, 1, 2, 3):
        chip = (y + by) % 4
        tiles.append((chip % 2) * 2 + chip // 2)
    return jnp.stack(tiles + [lax.axis_index("core")]).astype(jnp.int32)


def aligned(start, size):
    return pl.ds(pl.multiple_of(start, 128), size)


def local_call(kernel, out_shape, name, grant, cost, scratch=()):
    def call(tab, *args):
        return pl.pallas_call(
            kernel,
            out_shape=out_shape,
            in_specs=[pl.BlockSpec(memory_space=pltpu.SMEM)]
            + [pl.BlockSpec(memory_space=pltpu.VMEM)] * len(args),
            out_specs=jax.tree.map(lambda _: pl.BlockSpec(memory_space=pltpu.VMEM), out_shape),
            scratch_shapes=list(scratch),
            compiler_params=pltpu.CompilerParams(vmem_limit_bytes=grant << 20),
            cost_estimate=cost,
            name=name,
        )(tab, *args)

    return call


def moves(megabytes):
    return pl.CostEstimate(flops=0, transcendentals=0, bytes_accessed=int(megabytes * 2**20))


def array(*shape, dtype=jnp.bfloat16):
    return jax.ShapeDtypeStruct(shape, dtype)


def pack_kv_kernel(tab, k_ref, v_ref, *out):
    for i in range(4):
        at = tab[DST + i] * 512
        for n, src in enumerate((k_ref, v_ref)):
            for head in range(4):
                col = 256 * head + 128 * n
                out[i][:, col : col + 128] = src[:, aligned(at + 128 * head, 128)]


def pack_qd_kernel(tab, q_ref, d_ref, *out):
    for i in range(4):
        at = tab[DST + i] * 1024
        for n, src in enumerate((q_ref, d_ref)):
            for core in range(2):
                for chunk in range(2):
                    col = 512 * core + 256 * n
                    out[4 * chunk + i][:, col : col + 256] = src[
                        :, aligned(at + 512 * core + 256 * chunk, 256)
                    ]


def to_sibling_in_kernel(tab, p0, p1, p2, p3, out):
    at = (1 - tab[CORE]) * 512
    for i, p in enumerate((p0, p1, p2, p3)):
        out[i] = p[:, aligned(at, 512)]


def to_sibling_out_kernel(tab, p0, p1, p2, p3, out):
    at = (1 - tab[CORE]) * 128
    for i, p in enumerate((p0, p1, p2, p3)):
        out[i] = p[aligned(at, 128), :]


def halo_kernel(tab, p0, p1, p2, p3, sib, out0, out1):
    at = tab[CORE] * 512
    for chunk, out in enumerate((out0, out1)):
        for i, p in enumerate((p0, p1, p2, p3)):
            out[2 * i] = p[:, aligned(at + 256 * chunk, 256)]
            out[2 * i + 1] = sib[i, :, 256 * chunk : 256 * (chunk + 1)]


def merge_kernel(tab, own0, own1, from0, from1, *out):
    for i in range(4):
        rows = aligned(tab[DST + i] * TILE, TILE)
        for chunk, (own, other) in enumerate(((own0, from0), (own1, from1))):
            out[i][:, 256 * chunk : 256 * (chunk + 1)] = (
                own[rows, :] + other[rows, :].astype(jnp.float32)
            ).astype(jnp.bfloat16)


def arrived(tab, direct, sib):
    core = tab[CORE]
    for i in range(4):
        yield 2 * tab[SRC + i] + core, direct[i].at[aligned(core * 128, 128), :]
        yield 2 * tab[SRC + i] + 1 - core, sib.at[i]


def unpack_out_kernel(tab, *refs):
    o_ref, dq_ref = refs[10:]
    for chunk in range(2):
        parts = refs[5 * chunk : 5 * chunk + 5]
        for group, piece in arrived(tab, parts[:4], parts[4]):
            for n, out in enumerate((o_ref, dq_ref)):
                out[:, aligned(group * 512 + 256 * chunk, 256)] = piece[:, 256 * n : 256 * (n + 1)]


def unpack_kv_kernel(tab, p0, p1, p2, p3, sib, dk_ref, dv_ref):
    for group, piece in arrived(tab, (p0, p1, p2, p3), sib):
        for chunk in range(2):
            for n, out in enumerate((dk_ref, dv_ref)):
                at = 256 * chunk + 128 * n
                out[:, aligned(group * 256 + 128 * chunk, 128)] = piece[:, at : at + 128]


def attn_kernel(chunk, tab, bias_ref, *refs):
    q_parts, q_sib, kv_parts, kv_sib, halo = refs[0:4], refs[4], refs[5:9], refs[9], refs[10]
    outs, ghalo_ref, gown_ref = refs[11:15], refs[15], refs[16]
    (
        kaug, vaug, kt, v1t, qd_ref, out_ref, qaug, doaug, s_ref, e_ref, d_ref, dk_acc, dv_acc,
    ) = refs[17:]
    f32, bf16 = jnp.float32, jnp.bfloat16
    core = tab[CORE]

    lane = lax.broadcasted_iota(jnp.int32, (BLOCK, 128), 1)
    three = jnp.where(lane < 3, 1.0, 0.0).astype(bf16)

    def place_kv(at, k, v):
        rows = aligned(at, BLOCK)
        kaug[rows, 0:128] = k
        kaug[rows, 128:256] = jnp.where(lane == at // BLOCK, 1.0, 0.0).astype(bf16)
        vaug[rows, 0:128] = v
        vaug[rows, 128:256] = three
        kt[:, rows] = k.T
        v1t[0:128, rows] = v.T
        v1t[128:144, rows] = jnp.ones((16, BLOCK), bf16)

    for i in range(4):
        for n in range(2):
            at = tab[SRC + i] * TILE + (core if n == 0 else 1 - core) * BLOCK
            place_kv(at, halo[2 * i + n, :, 0:128], halo[2 * i + n, :, 128:256])
            if n == 0:
                col = core * 512 + 256 * chunk
                k = kv_parts[i][:, aligned(col, 128)]
                v = kv_parts[i][:, aligned(col + 128, 128)]
                qd = q_parts[i][:, aligned(core * 512, 512)]
            else:
                k = kv_sib[i, :, 256 * chunk : 256 * chunk + 128]
                v = kv_sib[i, :, 256 * chunk + 128 : 256 * chunk + 256]
                qd = q_sib[i]
            place_kv(SLAB + at, k, v)
            qd_ref[aligned(at, BLOCK), :] = qd
    dk_acc[...] = jnp.zeros_like(dk_acc)
    dv_acc[...] = jnp.zeros_like(dv_acc)

    @pl.loop(0, SLAB // TILE)
    def _(i):
        tile = pl.ds(pl.multiple_of(i * TILE, TILE), TILE)
        attn_tile(
            i, bias_ref, qd_ref.at[tile, :], out_ref.at[tile, :],
            kaug, vaug, kt, v1t, qaug, doaug, s_ref, e_ref, d_ref, dk_acc, dv_acc,
        )

    for i in range(4):
        outs[i][...] = out_ref[aligned(tab[DST + i] * TILE, TILE), :]
    ghalo_ref[:, 0:128] = (dk_acc[0:SLAB, :] * score_scale).astype(bf16)
    ghalo_ref[:, 128:256] = dv_acc[0:SLAB, :].astype(bf16)
    gown_ref[:, 0:128] = dk_acc[SLAB : 2 * SLAB, :] * score_scale
    gown_ref[:, 128:256] = dv_acc[SLAB : 2 * SLAB, :]


def attn_tile(
    i, bias_ref, qd_ref, out_ref,
    kaug, vaug, kt, v1t, qaug, doaug, s_ref, e_ref, d_ref, dk_acc, dv_acc,
):
    f32, bf16 = jnp.float32, jnp.bfloat16
    base = pl.multiple_of(i * TILE, TILE)
    window = pl.ds(base, 5 * TILE)

    for b in range(2):
        row_bias = bias_ref[pl.ds(2 * i + b, 1), :]
        rows_bias = jnp.broadcast_to(row_bias, (BLOCK, 128)).astype(bf16)
        for h in range(2):
            qaug[TILE * h + BLOCK * b : TILE * h + BLOCK * (b + 1), 128:256] = rows_bias
    for h in range(2):
        qaug[TILE * h : TILE * (h + 1), 0:128] = qd_ref[:, 128 * h : 128 * (h + 1)]

    s_pos = lax.broadcasted_iota(jnp.int32, (TILE, TILE), 0)
    t_pos = lax.broadcasted_iota(jnp.int32, (TILE, TILE), 1)
    far = s_pos > t_pos
    top8 = jnp.full((8, 2 * TILE), NEG, f32)
    for j in range(5):
        s = dot(kaug[pl.ds(base + TILE * j, TILE), :], qaug[...], NT)
        if j in (0, 4):
            keep = far if j == 0 else jnp.logical_not(far)
            s = jnp.concatenate(
                [jnp.where(keep, s[:, :TILE], NEG), jnp.where(keep, s[:, TILE:], NEG)], axis=1
            )
        s_ref[TILE * j : TILE * (j + 1), :] = s
        top8 = jnp.maximum(top8, jnp.max(s.reshape(TILE // 8, 8, 2 * TILE), axis=0))
    top = jnp.max(top8, axis=0, keepdims=True)
    for j in range(5):
        rows = slice(TILE * j, TILE * (j + 1))
        e_ref[rows, :] = jnp.exp2((s_ref[rows, :] - top) * exp2_scale).astype(bf16)

    ot = dot(v1t[:, window], e_ref[...])
    r = 1.0 / ot[128:129, :]
    attended = (ot[0:128, :] * r).T.astype(bf16)
    r_rows = jnp.broadcast_to(r, (128, 2 * TILE)).T
    grad = jnp.concatenate([qd_ref[:, 256:384], qd_ref[:, 384:512]], axis=0)
    grad_n = (grad.astype(f32) * r_rows).astype(bf16)
    delta = jnp.sum(grad_n.astype(f32) * attended.astype(f32), axis=1, keepdims=True)
    minus = jnp.broadcast_to(-delta, (2 * TILE, 128))
    part0 = minus.astype(bf16).astype(f32)
    part1 = (minus - part0).astype(bf16).astype(f32)
    part2 = minus - part0 - part1
    lane = lax.broadcasted_iota(jnp.int32, (2 * TILE, 128), 1)
    parts = jnp.where(
        lane == 0, part0, jnp.where(lane == 1, part1, jnp.where(lane == 2, part2, 0.0))
    )
    doaug[:, 0:128] = grad_n
    doaug[:, 128:256] = parts.astype(bf16)
    for h in range(2):
        out_ref[:, 128 * h : 128 * (h + 1)] = attended[TILE * h : TILE * (h + 1), :]

    for j in range(5):
        rows = slice(TILE * j, TILE * (j + 1))
        dp = dot(vaug[pl.ds(base + TILE * j, TILE), :], doaug[...], NT)
        d_ref[rows, :] = (e_ref[rows, :].astype(f32) * dp).astype(bf16)

    dq = (dot(kt[:, window], d_ref[...]) * score_scale).T.astype(bf16)
    for h in range(2):
        out_ref[:, 256 + 128 * h : 384 + 128 * h] = dq[TILE * h : TILE * (h + 1), :]
    dv = dot(e_ref[...], doaug[:, 0:128])
    dk = dot(d_ref[...], qaug[:, 0:128])

    dk_acc[window, :] = dk_acc[window, :] + dk
    dv_acc[window, :] = dv_acc[window, :] + dv


def attend(chunk, tab, bias, q_parts, q_sib, kv_parts, kv_sib, halo):
    f32, bf16 = jnp.float32, jnp.bfloat16
    call = local_call(
        functools.partial(attn_kernel, chunk),
        [array(TILE, 512)] * 4 + [array(SLAB, 256), array(SLAB, 256, dtype=f32)],
        f"attend_{chunk}",
        GRANT_ATTEND,
        pl.CostEstimate(flops=14 * 10**9, transcendentals=0, bytes_accessed=4 << 20),
        scratch=[
            pltpu.VMEM((2 * SLAB, 256), bf16),
            pltpu.VMEM((2 * SLAB, 256), bf16),
            pltpu.VMEM((128, 2 * SLAB), bf16),
            pltpu.VMEM((144, 2 * SLAB), bf16),
            pltpu.VMEM((SLAB, 512), bf16),
            pltpu.VMEM((SLAB, 512), bf16),
            pltpu.VMEM((2 * TILE, 256), bf16),
            pltpu.VMEM((2 * TILE, 256), bf16),
            pltpu.VMEM((5 * TILE, 2 * TILE), f32),
            pltpu.VMEM((5 * TILE, 2 * TILE), bf16),
            pltpu.VMEM((5 * TILE, 2 * TILE), bf16),
            pltpu.VMEM((2 * SLAB, 128), f32),
            pltpu.VMEM((2 * SLAB, 128), f32),
        ],
    )
    out = call(tab, bias, *q_parts, q_sib, *kv_parts, kv_sib, halo)
    return out[:4], out[4], out[5]


def block_bias(doc_ids, slab):
    blocks = SLAB // BLOCK
    padded = jnp.concatenate([jnp.full((SLAB,), -1, jnp.int32), doc_ids])
    ids = lax.dynamic_slice_in_dim(padded, slab * SLAB, 2 * SLAB, 0).reshape(2 * blocks, BLOCK)[:, 0]
    own = ids[blocks:]
    query = jnp.arange(blocks)[:, None]
    key = jnp.arange(2 * blocks)[None, :]
    ok = (own[:, None] == ids[None, :]) & (key >= query) & (key <= query + blocks)
    return jnp.pad(jnp.where(ok, 0.0, NEG).astype(jnp.float32), ((0, 0), (0, 128 - 2 * blocks)))


RING = ("y_lo", "y_hi", "core")
LINE = ("x", "z")


def ring_shift(x, by):
    pairs = []
    for device in range(8):
        y_lo, y_hi, core = device // 4, device // 2 % 2, device % 2
        chip = (2 * y_hi + y_lo + by) % 4
        pairs.append((device, (chip % 2) * 4 + (chip // 2) * 2 + core))
    return lax.ppermute(x, RING, pairs)


def spread(pieces):
    return [pieces[0]] + [ring_shift(pieces[i], i) for i in (1, 3, 2)]


def in_order(received):
    return [received[0], received[1], received[3], received[2]]


def exchange(pieces):
    return in_order(spread(pieces))


def swap_cores(x):
    return lax.ppermute(x, "core", [(0, 1), (1, 0)])


def shifted(x, by):
    count = lax.axis_size(LINE)
    pairs = [(i, i + by) for i in range(count) if 0 <= i + by < count]
    return lax.ppermute(x, LINE, pairs)


def body(queries, key_vectors, value_vectors, output_gradient, doc_ids):
    tab = scalars()
    rows = queries.shape[0]
    sibling_in = local_call(
        to_sibling_in_kernel, array(4, rows, 512), "to_sibling_in", GRANT, moves(1)
    )
    sibling_out = local_call(
        to_sibling_out_kernel, array(4, rows, 512), "to_sibling_out", GRANT, moves(1)
    )
    kv_send = local_call(
        pack_kv_kernel, [array(rows, 1024)] * 4, "pack_kv", GRANT, moves(2)
    )(tab, key_vectors, value_vectors)
    bias = block_bias(doc_ids, lax.axis_index(LINE))
    kv = exchange(kv_send)
    queries, _ = lax.optimization_barrier((queries, kv[1]))
    qd_send = local_call(
        pack_qd_kernel, [array(rows, 1024)] * 8, "pack_qd", GRANT, moves(4)
    )(tab, queries, output_gradient)
    kv, _, bias = lax.optimization_barrier((kv, qd_send, bias))
    kv_sib = swap_cores(sibling_in(tab, *kv))
    halo_send = local_call(
        halo_kernel, [array(8, rows, 256)] * 2, "halo", GRANT, moves(2)
    )(tab, *kv, kv_sib)
    halo = [shifted(x, 1) for x in halo_send]
    qd_send = [lax.optimization_barrier((qd_send[:4], halo_send))[0], lax.optimization_barrier((qd_send[4:], halo_send))[0]]
    received, own, other = [], [], []
    for chunk in range(2):
        qd = exchange(qd_send[chunk])
        if chunk == 1:
            qd, own = lax.optimization_barrier((qd, own))
        qd_sib = swap_cores(sibling_in(tab, *qd))
        pieces, g_halo, g_own = attend(chunk, tab, bias, qd, qd_sib, kv, kv_sib, halo[chunk])
        if chunk == 1:
            received[0], g_own = lax.optimization_barrier((received[0], g_own))
            sent = sibling_out(tab, *received[0])
            pieces, g_halo, _ = lax.optimization_barrier((pieces, g_halo, sent))
        received.append(exchange(pieces))
        own.append(g_own)
        other.append(shifted(g_halo, -1))
    out = [*received[0], swap_cores(sent), *received[1]]
    out.append(swap_cores(sibling_out(tab, *received[1])))
    attn_out, query_grad = local_call(
        unpack_out_kernel, [array(rows, 4096)] * 2, "unpack_out", GRANT, moves(4)
    )(tab, *out)
    pieces = local_call(merge_kernel, [array(TILE, 512)] * 4, "merge", GRANT, moves(4))(
        tab, *own, *other
    )
    received = exchange(pieces)
    key_grad, value_grad = local_call(
        unpack_kv_kernel, [array(rows, 2048)] * 2, "unpack_kv", GRANT, moves(2)
    )(tab, *received, swap_cores(sibling_out(tab, *received)))
    return attn_out, query_grad, key_grad, value_grad


def solution(mesh):
    seqa, seqb, head = (mesh.shape[a] for a in ("seqa", "seqb", "head"))
    axes = ("x", "z", "y_lo", "y_hi", "core")
    fine = Mesh(mesh.devices.reshape(seqa, seqb // 2, 2, head // 2, 2), axes)
    tokens = P(axes, None)
    return jax.shard_map(
        body, mesh=fine, in_specs=(tokens,) * 4 + (P(),), out_specs=(tokens,) * 4, check_vma=False
    )
```

```python
import functools

import jax
import jax.numpy as jnp
from jax import lax
from jax.experimental import pallas as pl
from jax.experimental.pallas import tpu as pltpu
from jax.sharding import Mesh, PartitionSpec as P

HEAD_SIZE = 128
BLOCK = 128
TILE = 256
SLAB = 1024
NEG = -1e30
GRANT = 12
GRANT_ATTEND = 28

score_scale = 168.0 ** (-0.5)
exp2_scale = score_scale * 1.4426950408889634

NT = (((1,), (1,)), ((), ()))
NN = (((1,), (0,)), ((), ()))


def dot(a, b, dims=NN):
    return lax.dot_general(a, b, dims, preferred_element_type=jnp.float32)


SRC, DST, CORE = 0, 4, 8


def scalars():
    y = lax.axis_index("y_hi") * 2 + lax.axis_index("y_lo")
    tiles = []
    for by in (0, -1, -2, -3, 0, 1, 2, 3):
        chip = (y + by) % 4
        tiles.append((chip % 2) * 2 + chip // 2)
    return jnp.stack(tiles + [lax.axis_index("core")]).astype(jnp.int32)


def aligned(start, size):
    return pl.ds(pl.multiple_of(start, 128), size)


def local_call(kernel, out_shape, name, grant, cost, scratch=()):
    def call(tab, *args):
        return pl.pallas_call(
            kernel,
            out_shape=out_shape,
            in_specs=[pl.BlockSpec(memory_space=pltpu.SMEM)]
            + [pl.BlockSpec(memory_space=pltpu.VMEM)] * len(args),
            out_specs=jax.tree.map(lambda _: pl.BlockSpec(memory_space=pltpu.VMEM), out_shape),
            scratch_shapes=list(scratch),
            compiler_params=pltpu.CompilerParams(vmem_limit_bytes=grant << 20),
            cost_estimate=cost,
            name=name,
        )(tab, *args)

    return call


def moves(megabytes):
    return pl.CostEstimate(flops=0, transcendentals=0, bytes_accessed=int(megabytes * 2**20))


def array(*shape, dtype=jnp.bfloat16):
    return jax.ShapeDtypeStruct(shape, dtype)


def pack_kv_kernel(tab, k_ref, v_ref, *out):
    for i in range(4):
        at = tab[DST + i] * 512
        for n, src in enumerate((k_ref, v_ref)):
            for head in range(4):
                col = 256 * head + 128 * n
                out[i][:, col : col + 128] = src[:, aligned(at + 128 * head, 128)]


def pack_qd_kernel(tab, q_ref, d_ref, *out):
    for i in range(4):
        at = tab[DST + i] * 1024
        for n, src in enumerate((q_ref, d_ref)):
            for core in range(2):
                for chunk in range(2):
                    col = 512 * core + 256 * n
                    out[4 * chunk + i][:, col : col + 256] = src[
                        :, aligned(at + 512 * core + 256 * chunk, 256)
                    ]


def to_sibling_in_kernel(tab, p0, p1, p2, p3, out):
    at = (1 - tab[CORE]) * 512
    for i, p in enumerate((p0, p1, p2, p3)):
        out[i] = p[:, aligned(at, 512)]


def to_sibling_out_kernel(tab, p0, p1, p2, p3, out):
    at = (1 - tab[CORE]) * 128
    for i, p in enumerate((p0, p1, p2, p3)):
        out[i] = p[aligned(at, 128), :]


def halo_kernel(tab, p0, p1, p2, p3, sib, out0, out1):
    at = tab[CORE] * 512
    for chunk, out in enumerate((out0, out1)):
        for i, p in enumerate((p0, p1, p2, p3)):
            out[2 * i] = p[:, aligned(at + 256 * chunk, 256)]
            out[2 * i + 1] = sib[i, :, 256 * chunk : 256 * (chunk + 1)]


def merge_kernel(tab, own0, own1, from0, from1, *out):
    for i in range(4):
        rows = aligned(tab[DST + i] * TILE, TILE)
        for chunk, (own, other) in enumerate(((own0, from0), (own1, from1))):
            out[i][:, 256 * chunk : 256 * (chunk + 1)] = (
                own[rows, :] + other[rows, :].astype(jnp.float32)
            ).astype(jnp.bfloat16)


def arrived(tab, direct, sib):
    core = tab[CORE]
    for i in range(4):
        yield 2 * tab[SRC + i] + core, direct[i].at[aligned(core * 128, 128), :]
        yield 2 * tab[SRC + i] + 1 - core, sib.at[i]


def unpack_out_kernel(tab, *refs):
    o_ref, dq_ref = refs[10:]
    for chunk in range(2):
        parts = refs[5 * chunk : 5 * chunk + 5]
        for group, piece in arrived(tab, parts[:4], parts[4]):
            for n, out in enumerate((o_ref, dq_ref)):
                out[:, aligned(group * 512 + 256 * chunk, 256)] = piece[:, 256 * n : 256 * (n + 1)]


def unpack_kv_kernel(tab, p0, p1, p2, p3, sib, dk_ref, dv_ref):
    for group, piece in arrived(tab, (p0, p1, p2, p3), sib):
        for chunk in range(2):
            for n, out in enumerate((dk_ref, dv_ref)):
                at = 256 * chunk + 128 * n
                out[:, aligned(group * 256 + 128 * chunk, 128)] = piece[:, at : at + 128]


def attn_kernel(chunk, tab, bias_ref, *refs):
    q_parts, q_sib, kv_parts, kv_sib, halo = refs[0:4], refs[4], refs[5:9], refs[9], refs[10]
    outs, ghalo_ref, gown_ref = refs[11:15], refs[15], refs[16]
    (
        kaug, vaug, kt, v1t, qd_ref, out_ref, qaug, doaug, s_ref, e_ref, d_ref, dk_acc, dv_acc,
    ) = refs[17:]
    f32, bf16 = jnp.float32, jnp.bfloat16
    core = tab[CORE]

    lane = lax.broadcasted_iota(jnp.int32, (BLOCK, 128), 1)
    three = jnp.where(lane < 3, 1.0, 0.0).astype(bf16)

    def place_kv(at, k, v):
        rows = aligned(at, BLOCK)
        kaug[rows, 0:128] = k
        kaug[rows, 128:256] = jnp.where(lane == at // BLOCK, 1.0, 0.0).astype(bf16)
        vaug[rows, 0:128] = v
        vaug[rows, 128:256] = three
        kt[:, rows] = k.T
        v1t[0:128, rows] = v.T
        v1t[128:144, rows] = jnp.ones((16, BLOCK), bf16)

    for i in range(4):
        for n in range(2):
            at = tab[SRC + i] * TILE + (core if n == 0 else 1 - core) * BLOCK
            place_kv(at, halo[2 * i + n, :, 0:128], halo[2 * i + n, :, 128:256])
            if n == 0:
                col = core * 512 + 256 * chunk
                k = kv_parts[i][:, aligned(col, 128)]
                v = kv_parts[i][:, aligned(col + 128, 128)]
                qd = q_parts[i][:, aligned(core * 512, 512)]
            else:
                k = kv_sib[i, :, 256 * chunk : 256 * chunk + 128]
                v = kv_sib[i, :, 256 * chunk + 128 : 256 * chunk + 256]
                qd = q_sib[i]
            place_kv(SLAB + at, k, v)
            qd_ref[aligned(at, BLOCK), :] = qd
    dk_acc[...] = jnp.zeros_like(dk_acc)
    dv_acc[...] = jnp.zeros_like(dv_acc)

    @pl.loop(0, SLAB // TILE)
    def _(i):
        tile = pl.ds(pl.multiple_of(i * TILE, TILE), TILE)
        attn_tile(
            i, bias_ref, qd_ref.at[tile, :], out_ref.at[tile, :],
            kaug, vaug, kt, v1t, qaug, doaug, s_ref, e_ref, d_ref, dk_acc, dv_acc,
        )

    for i in range(4):
        outs[i][...] = out_ref[aligned(tab[DST + i] * TILE, TILE), :]
    ghalo_ref[:, 0:128] = (dk_acc[0:SLAB, :] * score_scale).astype(bf16)
    ghalo_ref[:, 128:256] = dv_acc[0:SLAB, :].astype(bf16)
    gown_ref[:, 0:128] = dk_acc[SLAB : 2 * SLAB, :] * score_scale
    gown_ref[:, 128:256] = dv_acc[SLAB : 2 * SLAB, :]


def attn_tile(
    i, bias_ref, qd_ref, out_ref,
    kaug, vaug, kt, v1t, qaug, doaug, s_ref, e_ref, d_ref, dk_acc, dv_acc,
):
    f32, bf16 = jnp.float32, jnp.bfloat16
    base = pl.multiple_of(i * TILE, TILE)
    window = pl.ds(base, 5 * TILE)

    for b in range(2):
        row_bias = bias_ref[pl.ds(2 * i + b, 1), :]
        rows_bias = jnp.broadcast_to(row_bias, (BLOCK, 128)).astype(bf16)
        for h in range(2):
            qaug[TILE * h + BLOCK * b : TILE * h + BLOCK * (b + 1), 128:256] = rows_bias
    for h in range(2):
        qaug[TILE * h : TILE * (h + 1), 0:128] = qd_ref[:, 128 * h : 128 * (h + 1)]

    s_pos = lax.broadcasted_iota(jnp.int32, (TILE, TILE), 0)
    t_pos = lax.broadcasted_iota(jnp.int32, (TILE, TILE), 1)
    far = s_pos > t_pos
    heads = [slice(TILE * h, TILE * (h + 1)) for h in range(2)]
    steps = [slice(TILE * j, TILE * (j + 1)) for j in range(5)]

    def score(h, j, top8):
        s = dot(kaug[pl.ds(base + TILE * j, TILE), :], qaug[heads[h], :], NT)
        if j == 0:
            s = jnp.where(far, s, NEG)
        if j == 4:
            s = jnp.where(far, NEG, s)
        s_ref[steps[j], heads[h]] = s
        return jnp.maximum(top8, jnp.max(s.reshape(TILE // 8, 8, TILE), axis=0))

    def exponentiate(h, j, top):
        e_ref[steps[j], heads[h]] = jnp.exp2(
            (s_ref[steps[j], heads[h]] - top) * exp2_scale
        ).astype(bf16)

    def normalize(h, ot):
        r = 1.0 / ot[128:129, :]
        attended = (ot[0:128, :] * r).T.astype(bf16)
        out_ref[:, 128 * h : 128 * (h + 1)] = attended
        r_rows = jnp.broadcast_to(r, (128, TILE)).T
        grad = qd_ref[:, 256 + 128 * h : 384 + 128 * h]
        grad_n = (grad.astype(f32) * r_rows).astype(bf16)
        delta = jnp.sum(grad_n.astype(f32) * attended.astype(f32), axis=1, keepdims=True)
        minus = jnp.broadcast_to(-delta, (TILE, 128))
        part0 = minus.astype(bf16).astype(f32)
        part1 = (minus - part0).astype(bf16).astype(f32)
        part2 = minus - part0 - part1
        lane = lax.broadcasted_iota(jnp.int32, (TILE, 128), 1)
        parts = jnp.where(
            lane == 0, part0, jnp.where(lane == 1, part1, jnp.where(lane == 2, part2, 0.0))
        )
        doaug[heads[h], 0:128] = grad_n
        doaug[heads[h], 128:256] = parts.astype(bf16)

    def score_gradient(h, j):
        dp = dot(vaug[pl.ds(base + TILE * j, TILE), :], doaug[heads[h], :], NT)
        d_ref[steps[j], heads[h]] = (e_ref[steps[j], heads[h]].astype(f32) * dp).astype(bf16)

    def query_gradient(h):
        dq = (dot(kt[:, window], d_ref[:, heads[h]]) * score_scale).T.astype(bf16)
        out_ref[:, 256 + 128 * h : 384 + 128 * h] = dq

    lowest = jnp.full((8, TILE), NEG, f32)
    top8 = lowest
    for j in range(5):
        top8 = score(0, j, top8)
    top0 = jnp.max(top8, axis=0, keepdims=True)
    top8 = lowest
    for j in range(5):
        top8 = score(1, j, top8)
        exponentiate(0, j, top0)
    top1 = jnp.max(top8, axis=0, keepdims=True)
    ot0 = dot(v1t[:, window], e_ref[:, heads[0]])
    for j in range(5):
        exponentiate(1, j, top1)
    normalize(0, ot0)
    ot1 = dot(v1t[:, window], e_ref[:, heads[1]])
    for j in range(5):
        score_gradient(0, j)
    normalize(1, ot1)
    query_gradient(0)
    for j in range(5):
        score_gradient(1, j)
    dv = dot(e_ref[...], doaug[:, 0:128])
    query_gradient(1)
    dk = dot(d_ref[...], qaug[:, 0:128])

    dk_acc[window, :] = dk_acc[window, :] + dk
    dv_acc[window, :] = dv_acc[window, :] + dv


def attend(chunk, tab, bias, q_parts, q_sib, kv_parts, kv_sib, halo):
    f32, bf16 = jnp.float32, jnp.bfloat16
    call = local_call(
        functools.partial(attn_kernel, chunk),
        [array(TILE, 512)] * 4 + [array(SLAB, 256), array(SLAB, 256, dtype=f32)],
        f"attend_{chunk}",
        GRANT_ATTEND,
        pl.CostEstimate(flops=14 * 10**9, transcendentals=0, bytes_accessed=4 << 20),
        scratch=[
            pltpu.VMEM((2 * SLAB, 256), bf16),
            pltpu.VMEM((2 * SLAB, 256), bf16),
            pltpu.VMEM((128, 2 * SLAB), bf16),
            pltpu.VMEM((144, 2 * SLAB), bf16),
            pltpu.VMEM((SLAB, 512), bf16),
            pltpu.VMEM((SLAB, 512), bf16),
            pltpu.VMEM((2 * TILE, 256), bf16),
            pltpu.VMEM((2 * TILE, 256), bf16),
            pltpu.VMEM((5 * TILE, 2 * TILE), f32),
            pltpu.VMEM((5 * TILE, 2 * TILE), bf16),
            pltpu.VMEM((5 * TILE, 2 * TILE), bf16),
            pltpu.VMEM((2 * SLAB, 128), f32),
            pltpu.VMEM((2 * SLAB, 128), f32),
        ],
    )
    out = call(tab, bias, *q_parts, q_sib, *kv_parts, kv_sib, halo)
    return out[:4], out[4], out[5]


def block_bias(doc_ids, slab):
    blocks = SLAB // BLOCK
    padded = jnp.concatenate([jnp.full((SLAB,), -1, jnp.int32), doc_ids])
    ids = lax.dynamic_slice_in_dim(padded, slab * SLAB, 2 * SLAB, 0).reshape(2 * blocks, BLOCK)[:, 0]
    own = ids[blocks:]
    query = jnp.arange(blocks)[:, None]
    key = jnp.arange(2 * blocks)[None, :]
    ok = (own[:, None] == ids[None, :]) & (key >= query) & (key <= query + blocks)
    return jnp.pad(jnp.where(ok, 0.0, NEG).astype(jnp.float32), ((0, 0), (0, 128 - 2 * blocks)))


RING = ("y_lo", "y_hi", "core")
LINE = ("x", "z")


def ring_shift(x, by):
    pairs = []
    for device in range(8):
        y_lo, y_hi, core = device // 4, device // 2 % 2, device % 2
        chip = (2 * y_hi + y_lo + by) % 4
        pairs.append((device, (chip % 2) * 4 + (chip // 2) * 2 + core))
    return lax.ppermute(x, RING, pairs)


def spread(pieces):
    return [pieces[0]] + [ring_shift(pieces[i], i) for i in (1, 3, 2)]


def in_order(received):
    return [received[0], received[1], received[3], received[2]]


def exchange(pieces):
    return in_order(spread(pieces))


def swap_cores(x):
    return lax.ppermute(x, "core", [(0, 1), (1, 0)])


def shifted(x, by):
    count = lax.axis_size(LINE)
    pairs = [(i, i + by) for i in range(count) if 0 <= i + by < count]
    return lax.ppermute(x, LINE, pairs)


def body(queries, key_vectors, value_vectors, output_gradient, doc_ids):
    tab = scalars()
    rows = queries.shape[0]
    sibling_in = local_call(
        to_sibling_in_kernel, array(4, rows, 512), "to_sibling_in", GRANT, moves(1)
    )
    sibling_out = local_call(
        to_sibling_out_kernel, array(4, rows, 512), "to_sibling_out", GRANT, moves(1)
    )
    kv_send = local_call(
        pack_kv_kernel, [array(rows, 1024)] * 4, "pack_kv", GRANT, moves(2)
    )(tab, key_vectors, value_vectors)
    bias = block_bias(doc_ids, lax.axis_index(LINE))
    kv = exchange(kv_send)
    queries, _ = lax.optimization_barrier((queries, kv[1]))
    qd_send = local_call(
        pack_qd_kernel, [array(rows, 1024)] * 8, "pack_qd", GRANT, moves(4)
    )(tab, queries, output_gradient)
    kv, _, bias = lax.optimization_barrier((kv, qd_send, bias))
    kv_sib = swap_cores(sibling_in(tab, *kv))
    halo_send = local_call(
        halo_kernel, [array(8, rows, 256)] * 2, "halo", GRANT, moves(2)
    )(tab, *kv, kv_sib)
    halo = [shifted(x, 1) for x in halo_send]
    qd_send = [lax.optimization_barrier((qd_send[:4], halo_send))[0], lax.optimization_barrier((qd_send[4:], halo_send))[0]]
    received, own, other = [], [], []
    for chunk in range(2):
        qd = exchange(qd_send[chunk])
        if chunk == 1:
            qd, own = lax.optimization_barrier((qd, own))
        qd_sib = swap_cores(sibling_in(tab, *qd))
        pieces, g_halo, g_own = attend(chunk, tab, bias, qd, qd_sib, kv, kv_sib, halo[chunk])
        if chunk == 1:
            received[0], g_own = lax.optimization_barrier((received[0], g_own))
            sent = sibling_out(tab, *received[0])
            pieces, g_halo, _ = lax.optimization_barrier((pieces, g_halo, sent))
        received.append(exchange(pieces))
        own.append(g_own)
        other.append(shifted(g_halo, -1))
    out = [*received[0], swap_cores(sent), *received[1]]
    out.append(swap_cores(sibling_out(tab, *received[1])))
    attn_out, query_grad = local_call(
        unpack_out_kernel, [array(rows, 4096)] * 2, "unpack_out", GRANT, moves(4)
    )(tab, *out)
    pieces = local_call(merge_kernel, [array(TILE, 512)] * 4, "merge", GRANT, moves(4))(
        tab, *own, *other
    )
    received = exchange(pieces)
    key_grad, value_grad = local_call(
        unpack_kv_kernel, [array(rows, 2048)] * 2, "unpack_kv", GRANT, moves(2)
    )(tab, *received, swap_cores(sibling_out(tab, *received)))
    return attn_out, query_grad, key_grad, value_grad


def solution(mesh):
    seqa, seqb, head = (mesh.shape[a] for a in ("seqa", "seqb", "head"))
    axes = ("x", "z", "y_lo", "y_hi", "core")
    fine = Mesh(mesh.devices.reshape(seqa, seqb // 2, 2, head // 2, 2), axes)
    tokens = P(axes, None)
    return jax.shard_map(
        body, mesh=fine, in_specs=(tokens,) * 4 + (P(),), out_specs=(tokens,) * 4, check_vma=False
    )
```

```python
import functools

import jax
import jax.numpy as jnp
from jax import lax
from jax.experimental import pallas as pl
from jax.experimental.pallas import tpu as pltpu
from jax.sharding import Mesh, PartitionSpec as P

HEAD_SIZE = 128
BLOCK = 128
TILE = 256
SLAB = 1024
NEG = -1e30
GRANT = 12
GRANT_ATTEND = 28

score_scale = 168.0 ** (-0.5)
exp2_scale = score_scale * 1.4426950408889634

NT = (((1,), (1,)), ((), ()))
NN = (((1,), (0,)), ((), ()))


def dot(a, b, dims=NN):
    return lax.dot_general(a, b, dims, preferred_element_type=jnp.float32)


SRC, DST, CORE = 0, 4, 8


def scalars():
    y = lax.axis_index("y_hi") * 2 + lax.axis_index("y_lo")
    tiles = []
    for by in (0, -1, -2, -3, 0, 1, 2, 3):
        chip = (y + by) % 4
        tiles.append((chip % 2) * 2 + chip // 2)
    return jnp.stack(tiles + [lax.axis_index("core")]).astype(jnp.int32)


def aligned(start, size):
    return pl.ds(pl.multiple_of(start, 128), size)


def local_call(kernel, out_shape, name, grant, cost, scratch=()):
    def call(tab, *args):
        return pl.pallas_call(
            kernel,
            out_shape=out_shape,
            in_specs=[pl.BlockSpec(memory_space=pltpu.SMEM)]
            + [pl.BlockSpec(memory_space=pltpu.VMEM)] * len(args),
            out_specs=jax.tree.map(lambda _: pl.BlockSpec(memory_space=pltpu.VMEM), out_shape),
            scratch_shapes=list(scratch),
            compiler_params=pltpu.CompilerParams(vmem_limit_bytes=grant << 20),
            cost_estimate=cost,
            name=name,
        )(tab, *args)

    return call


def moves(megabytes):
    return pl.CostEstimate(flops=0, transcendentals=0, bytes_accessed=int(megabytes * 2**20))


def array(*shape, dtype=jnp.bfloat16):
    return jax.ShapeDtypeStruct(shape, dtype)


def pack_kv_kernel(tab, k_ref, v_ref, *out):
    for i in range(4):
        at = tab[DST + i] * 512
        for n, src in enumerate((k_ref, v_ref)):
            for head in range(4):
                col = 256 * head + 128 * n
                out[i][:, col : col + 128] = src[:, aligned(at + 128 * head, 128)]


def pack_qd_kernel(tab, q_ref, d_ref, *out):
    for i in range(4):
        at = tab[DST + i] * 1024
        for n, src in enumerate((q_ref, d_ref)):
            for core in range(2):
                for chunk in range(2):
                    col = 512 * core + 256 * n
                    out[4 * chunk + i][:, col : col + 256] = src[
                        :, aligned(at + 512 * core + 256 * chunk, 256)
                    ]


def to_sibling_in_kernel(tab, p0, p1, p2, p3, out):
    at = (1 - tab[CORE]) * 512
    for i, p in enumerate((p0, p1, p2, p3)):
        out[i] = p[:, aligned(at, 512)]


def to_sibling_out_kernel(tab, p0, p1, p2, p3, out):
    at = (1 - tab[CORE]) * 128
    for i, p in enumerate((p0, p1, p2, p3)):
        out[i] = p[aligned(at, 128), :]


def halo_kernel(tab, p0, p1, p2, p3, sib, out0, out1):
    at = tab[CORE] * 512
    for chunk, out in enumerate((out0, out1)):
        for i, p in enumerate((p0, p1, p2, p3)):
            out[2 * i] = p[:, aligned(at + 256 * chunk, 256)]
            out[2 * i + 1] = sib[i, :, 256 * chunk : 256 * (chunk + 1)]


def merge_kernel(tab, own0, own1, from0, from1, *out):
    for i in range(4):
        rows = aligned(tab[DST + i] * TILE, TILE)
        for chunk, (own, other) in enumerate(((own0, from0), (own1, from1))):
            out[i][:, 256 * chunk : 256 * (chunk + 1)] = (
                own[rows, :] + other[rows, :].astype(jnp.float32)
            ).astype(jnp.bfloat16)


def arrived(tab, direct, sib):
    core = tab[CORE]
    for i in range(4):
        yield 2 * tab[SRC + i] + core, direct[i].at[aligned(core * 128, 128), :]
        yield 2 * tab[SRC + i] + 1 - core, sib.at[i]


def unpack_out_kernel(tab, *refs):
    o_ref, dq_ref = refs[10:]
    for chunk in range(2):
        parts = refs[5 * chunk : 5 * chunk + 5]
        for group, piece in arrived(tab, parts[:4], parts[4]):
            for n, out in enumerate((o_ref, dq_ref)):
                out[:, aligned(group * 512 + 256 * chunk, 256)] = piece[:, 256 * n : 256 * (n + 1)]


def unpack_kv_kernel(tab, p0, p1, p2, p3, sib, dk_ref, dv_ref):
    for group, piece in arrived(tab, (p0, p1, p2, p3), sib):
        for chunk in range(2):
            for n, out in enumerate((dk_ref, dv_ref)):
                at = 256 * chunk + 128 * n
                out[:, aligned(group * 256 + 128 * chunk, 128)] = piece[:, at : at + 128]


def attn_kernel(chunk, tab, bias_ref, *refs):
    q_parts, q_sib, kv_parts, kv_sib, halo = refs[0:4], refs[4], refs[5:9], refs[9], refs[10]
    outs, ghalo_ref, gown_ref = refs[11:15], refs[15], refs[16]
    (
        kaug, vaug, kt, v1t, qd_ref, out_ref, qaug, doaug, s_ref, e_ref, d_ref, dk_acc, dv_acc,
    ) = refs[17:]
    f32, bf16 = jnp.float32, jnp.bfloat16
    core = tab[CORE]

    lane = lax.broadcasted_iota(jnp.int32, (BLOCK, 128), 1)
    three = jnp.where(lane < 3, 1.0, 0.0).astype(bf16)

    def place_kv(at, k, v):
        rows = aligned(at, BLOCK)
        kaug[rows, 0:128] = k
        kaug[rows, 128:256] = jnp.where(lane == at // BLOCK, 1.0, 0.0).astype(bf16)
        vaug[rows, 0:128] = v
        vaug[rows, 128:256] = three
        kt[:, rows] = k.T
        v1t[0:128, rows] = v.T
        v1t[128:144, rows] = jnp.ones((16, BLOCK), bf16)

    for i in range(4):
        for n in range(2):
            at = tab[SRC + i] * TILE + (core if n == 0 else 1 - core) * BLOCK
            place_kv(at, halo[2 * i + n, :, 0:128], halo[2 * i + n, :, 128:256])
            if n == 0:
                col = core * 512 + 256 * chunk
                k = kv_parts[i][:, aligned(col, 128)]
                v = kv_parts[i][:, aligned(col + 128, 128)]
                qd = q_parts[i][:, aligned(core * 512, 512)]
            else:
                k = kv_sib[i, :, 256 * chunk : 256 * chunk + 128]
                v = kv_sib[i, :, 256 * chunk + 128 : 256 * chunk + 256]
                qd = q_sib[i]
            place_kv(SLAB + at, k, v)
            qd_ref[aligned(at, BLOCK), :] = qd
    dk_acc[...] = jnp.zeros_like(dk_acc)
    dv_acc[...] = jnp.zeros_like(dv_acc)

    @pl.loop(0, SLAB // TILE)
    def _(i):
        tile = pl.ds(pl.multiple_of(i * TILE, TILE), TILE)
        attn_tile(
            i, bias_ref, qd_ref.at[tile, :], out_ref.at[tile, :],
            kaug, vaug, kt, v1t, qaug, doaug, s_ref, e_ref, d_ref, dk_acc, dv_acc,
        )

    for i in range(4):
        outs[i][...] = out_ref[aligned(tab[DST + i] * TILE, TILE), :]
    ghalo_ref[:, 0:128] = (dk_acc[0:SLAB, :] * score_scale).astype(bf16)
    ghalo_ref[:, 128:256] = dv_acc[0:SLAB, :].astype(bf16)
    gown_ref[:, 0:128] = dk_acc[SLAB : 2 * SLAB, :] * score_scale
    gown_ref[:, 128:256] = dv_acc[SLAB : 2 * SLAB, :]


def attn_tile(
    i, bias_ref, qd_ref, out_ref,
    kaug, vaug, kt, v1t, qaug, doaug, s_ref, e_ref, d_ref, dk_acc, dv_acc,
):
    f32, bf16 = jnp.float32, jnp.bfloat16
    base = pl.multiple_of(i * TILE, TILE)
    window = pl.ds(base, 5 * TILE)

    for b in range(2):
        row_bias = bias_ref[pl.ds(2 * i + b, 1), :]
        rows_bias = jnp.broadcast_to(row_bias, (BLOCK, 128)).astype(bf16)
        for h in range(2):
            qaug[TILE * h + BLOCK * b : TILE * h + BLOCK * (b + 1), 128:256] = rows_bias
    for h in range(2):
        qaug[TILE * h : TILE * (h + 1), 0:128] = qd_ref[:, 128 * h : 128 * (h + 1)]

    s_pos = lax.broadcasted_iota(jnp.int32, (TILE, TILE), 0)
    t_pos = lax.broadcasted_iota(jnp.int32, (TILE, TILE), 1)
    far = s_pos > t_pos
    heads = [slice(TILE * h, TILE * (h + 1)) for h in range(2)]
    steps = [slice(TILE * j, TILE * (j + 1)) for j in range(5)]

    def score(h, j, top8):
        s = dot(kaug[pl.ds(base + TILE * j, TILE), :], qaug[heads[h], :], NT)
        if j == 0:
            s = jnp.where(far, s, NEG)
        if j == 4:
            s = jnp.where(far, NEG, s)
        s_ref[steps[j], heads[h]] = s
        return jnp.maximum(top8, jnp.max(s.reshape(TILE // 8, 8, TILE), axis=0))

    def exponentiate(h, j, top):
        e_ref[steps[j], heads[h]] = jnp.exp2(
            (s_ref[steps[j], heads[h]] - top) * exp2_scale
        ).astype(bf16)

    def normalize(h, ot):
        r = 1.0 / ot[128:129, :]
        attended = (ot[0:128, :] * r).T.astype(bf16)
        out_ref[:, 128 * h : 128 * (h + 1)] = attended
        r_rows = jnp.broadcast_to(r, (128, TILE)).T
        grad = qd_ref[:, 256 + 128 * h : 384 + 128 * h]
        grad_n = (grad.astype(f32) * r_rows).astype(bf16)
        delta = jnp.sum(grad_n.astype(f32) * attended.astype(f32), axis=1, keepdims=True)
        minus = jnp.broadcast_to(-delta, (TILE, 128))
        part0 = minus.astype(bf16).astype(f32)
        part1 = (minus - part0).astype(bf16).astype(f32)
        part2 = minus - part0 - part1
        lane = lax.broadcasted_iota(jnp.int32, (TILE, 128), 1)
        parts = jnp.where(
            lane == 0, part0, jnp.where(lane == 1, part1, jnp.where(lane == 2, part2, 0.0))
        )
        doaug[heads[h], 0:128] = grad_n
        doaug[heads[h], 128:256] = parts.astype(bf16)

    def score_gradient(h, j):
        dp = dot(vaug[pl.ds(base + TILE * j, TILE), :], doaug[heads[h], :], NT)
        d_ref[steps[j], heads[h]] = (e_ref[steps[j], heads[h]].astype(f32) * dp).astype(bf16)

    def query_gradient(h):
        dq = (dot(kt[:, window], d_ref[:, heads[h]]) * score_scale).T.astype(bf16)
        out_ref[:, 256 + 128 * h : 384 + 128 * h] = dq

    lowest = jnp.full((8, TILE), NEG, f32)
    top8 = lowest
    for j in range(5):
        top8 = score(0, j, top8)
    top0 = jnp.max(top8, axis=0, keepdims=True)
    top8 = lowest
    for j in range(5):
        top8 = score(1, j, top8)
        exponentiate(0, j, top0)
    top1 = jnp.max(top8, axis=0, keepdims=True)
    ot0 = dot(v1t[:, window], e_ref[:, heads[0]])
    for j in range(5):
        exponentiate(1, j, top1)
    normalize(0, ot0)
    ot1 = dot(v1t[:, window], e_ref[:, heads[1]])
    for j in range(5):
        score_gradient(0, j)
    normalize(1, ot1)
    query_gradient(0)
    for j in range(5):
        score_gradient(1, j)
    dv = dot(e_ref[...], doaug[:, 0:128])
    query_gradient(1)
    dk = dot(d_ref[...], qaug[:, 0:128])

    dk_acc[window, :] = dk_acc[window, :] + dk
    dv_acc[window, :] = dv_acc[window, :] + dv


def attend(chunk, tab, bias, q_parts, q_sib, kv_parts, kv_sib, halo):
    f32, bf16 = jnp.float32, jnp.bfloat16
    call = local_call(
        functools.partial(attn_kernel, chunk),
        [array(TILE, 512)] * 4 + [array(SLAB, 256), array(SLAB, 256, dtype=f32)],
        f"attend_{chunk}",
        GRANT_ATTEND,
        pl.CostEstimate(flops=14 * 10**9, transcendentals=0, bytes_accessed=4 << 20),
        scratch=[
            pltpu.VMEM((2 * SLAB, 256), bf16),
            pltpu.VMEM((2 * SLAB, 256), bf16),
            pltpu.VMEM((128, 2 * SLAB), bf16),
            pltpu.VMEM((144, 2 * SLAB), bf16),
            pltpu.VMEM((SLAB, 512), bf16),
            pltpu.VMEM((SLAB, 512), bf16),
            pltpu.VMEM((2 * TILE, 256), bf16),
            pltpu.VMEM((2 * TILE, 256), bf16),
            pltpu.VMEM((5 * TILE, 2 * TILE), f32),
            pltpu.VMEM((5 * TILE, 2 * TILE), bf16),
            pltpu.VMEM((5 * TILE, 2 * TILE), bf16),
            pltpu.VMEM((2 * SLAB, 128), f32),
            pltpu.VMEM((2 * SLAB, 128), f32),
        ],
    )
    out = call(tab, bias, *q_parts, q_sib, *kv_parts, kv_sib, halo)
    return out[:4], out[4], out[5]


def block_bias(doc_ids, slab):
    blocks = SLAB // BLOCK
    padded = jnp.concatenate([jnp.full((SLAB,), -1, jnp.int32), doc_ids])
    ids = lax.dynamic_slice_in_dim(padded, slab * SLAB, 2 * SLAB, 0).reshape(2 * blocks, BLOCK)[:, 0]
    own = ids[blocks:]
    query = jnp.arange(blocks)[:, None]
    key = jnp.arange(2 * blocks)[None, :]
    ok = (own[:, None] == ids[None, :]) & (key >= query) & (key <= query + blocks)
    return jnp.pad(jnp.where(ok, 0.0, NEG).astype(jnp.float32), ((0, 0), (0, 128 - 2 * blocks)))


RING = ("y_lo", "y_hi", "core")
LINE = ("x", "z")


def ring_shift(x, by):
    pairs = []
    for device in range(8):
        y_lo, y_hi, core = device // 4, device // 2 % 2, device % 2
        chip = (2 * y_hi + y_lo + by) % 4
        pairs.append((device, (chip % 2) * 4 + (chip // 2) * 2 + core))
    return lax.ppermute(x, RING, pairs)


def spread(pieces):
    return [pieces[0]] + [ring_shift(pieces[i], i) for i in (1, 3, 2)]


def in_order(received):
    return [received[0], received[1], received[3], received[2]]


def exchange(pieces):
    return in_order(spread(pieces))


def swap_cores(x):
    return lax.ppermute(x, "core", [(0, 1), (1, 0)])


def shifted(x, by):
    count = lax.axis_size(LINE)
    pairs = [(i, i + by) for i in range(count) if 0 <= i + by < count]
    return lax.ppermute(x, LINE, pairs)


def body(queries, key_vectors, value_vectors, output_gradient, doc_ids):
    tab = scalars()
    rows = queries.shape[0]
    sibling_in = local_call(
        to_sibling_in_kernel, array(4, rows, 512), "to_sibling_in", GRANT, moves(1)
    )
    sibling_out = local_call(
        to_sibling_out_kernel, array(4, rows, 512), "to_sibling_out", GRANT, moves(1)
    )
    kv_send = local_call(
        pack_kv_kernel, [array(rows, 1024)] * 4, "pack_kv", GRANT, moves(2)
    )(tab, key_vectors, value_vectors)
    bias = block_bias(doc_ids, lax.axis_index(LINE))
    kv = exchange(kv_send)
    queries, _ = lax.optimization_barrier((queries, kv[1]))
    qd_send = local_call(
        pack_qd_kernel, [array(rows, 1024)] * 8, "pack_qd", GRANT, moves(4)
    )(tab, queries, output_gradient)
    kv, _, bias = lax.optimization_barrier((kv, qd_send, bias))
    kv_sib = swap_cores(sibling_in(tab, *kv))
    halo_send = local_call(
        halo_kernel, [array(8, rows, 256)] * 2, "halo", GRANT, moves(2)
    )(tab, *kv, kv_sib)
    halo = [shifted(x, 1) for x in halo_send]
    qd_send = [lax.optimization_barrier((qd_send[:4], halo_send))[0], lax.optimization_barrier((qd_send[4:], halo_send))[0]]
    received, own, other = [], [], []
    for chunk in range(2):
        qd = exchange(qd_send[chunk])
        if chunk == 1:
            qd, own = lax.optimization_barrier((qd, own))
        qd_sib = swap_cores(sibling_in(tab, *qd))
        pieces, g_halo, g_own = attend(chunk, tab, bias, qd, qd_sib, kv, kv_sib, halo[chunk])
        if chunk == 1:
            received[0], g_own = lax.optimization_barrier((received[0], g_own))
            sent = sibling_out(tab, *received[0])
            pieces, _ = lax.optimization_barrier((pieces, sent))
        received.append(exchange(pieces))
        own.append(g_own)
        other.append(shifted(g_halo, -1))
    out = [*received[0], swap_cores(sent), *received[1]]
    out.append(swap_cores(sibling_out(tab, *received[1])))
    attn_out, query_grad = local_call(
        unpack_out_kernel, [array(rows, 4096)] * 2, "unpack_out", GRANT, moves(4)
    )(tab, *out)
    pieces = local_call(merge_kernel, [array(TILE, 512)] * 4, "merge", GRANT, moves(4))(
        tab, *own, *other
    )
    received = exchange(pieces)
    key_grad, value_grad = local_call(
        unpack_kv_kernel, [array(rows, 2048)] * 2, "unpack_kv", GRANT, moves(2)
    )(tab, *received, swap_cores(sibling_out(tab, *received)))
    return attn_out, query_grad, key_grad, value_grad


def solution(mesh):
    seqa, seqb, head = (mesh.shape[a] for a in ("seqa", "seqb", "head"))
    axes = ("x", "z", "y_lo", "y_hi", "core")
    fine = Mesh(mesh.devices.reshape(seqa, seqb // 2, 2, head // 2, 2), axes)
    tokens = P(axes, None)
    return jax.shard_map(
        body, mesh=fine, in_specs=(tokens,) * 4 + (P(),), out_specs=(tokens,) * 4, check_vma=False
    )
```
